128 devices in a mesh: recv: 32 (over y, x_lo, z), depth: 4 (over x_hi, core).
Axes of the slice: x: 4 (x_hi: 2, x_lo: 2; x = x_hi * 2 + x_lo), y: 4, z: 4, core: 2. Of those that a mesh axis runs over, the one named last changes fastest.
Arguments:
- displace: bfloat16 [4, 32, 2, 8, 32, 128], P(None, 'recv', None, None, 'depth'), may hold values from -6 to 6
- green: bfloat16 [128, 2, 2, 8, 32, 128], P('recv', None, None, None, 'depth'), may hold values from -6 to 6
- pair_src: int32 [4, 128], P(None, 'recv'), may hold values from 0 to 31
- source_at: int32 [4, 32], replicated, may hold values from 0 to 31, each once within a row
Outputs:
- kernels: bfloat16 [4, 128, 2, 2, 9, 32, 128], P(None, 'recv', None, None, None, 'depth')
The draws below stay inside these ranges and needn't reach their ends.
Inputs may be any that keep to these rules, and one draw needn't show every extreme that they name: `source_at`: each row is a permutation of the slots.
All inputs are finite; a program needn't handle non-finite values.
Results may differ from the reference program's by a relative error of at most 0.0058.
Values may be sent and summed in bfloat16 or wider, within the bound.
No kernel may reach another device: no remote copies, remote signals or barrier semaphores. Data moves between devices by JAX's collectives and lax.ppermute only.
A program may use at most 128 MiB of HBM per device.

```python
import math
import jax
import jax.numpy as jnp
import numpy as np
from jax import lax

NH = 128
STEPS = 8
LAGS = 9
ROUNDS = 4
NSRC = 32
NREC = 128
NZ = 32


def set_ends(drawn, key, low, largest):
    extent = drawn.shape
    index_at = [jax.random.randint(jax.random.fold_in(key, axis), (), 0, extent[axis]) for axis in range(len(extent))]
    drawn = drawn.at[tuple(index_at)].set(low)
    longest = extent.index(max(extent))
    index_at[longest] = (index_at[longest] + 1) % extent[longest]
    return drawn.at[tuple(index_at)].set(largest)


def levels(own_key, extent, pieces, least, largest):
    def one(dim, shards_of):
        steps = jax.random.uniform(jax.random.fold_in(jax.random.fold_in(own_key, 6), dim), (shards_of,), jnp.float32, least / len(pieces), largest / len(pieces))
        return jnp.repeat(jnp.exp(steps), extent[dim] // shards_of).reshape((-1,) + (1,) * (len(extent) - dim - 1))

    gain = one(*pieces[0])
    for cut in pieces[1:]:
        gain = gain * one(*cut)
    return gain


def rank_bounds(number_of, slope):
    weights = [(1 << 20) // math.isqrt(grade ** slope) + 1 for grade in range(1, number_of + 1)]
    spread = 1 + sum(weights) // (1 << 30)
    return np.cumsum(np.array([max(1, weight // spread) for weight in weights]))


def skewed_ids(stream_key, dims, count, lean):
    grid = rank_bounds(count, lean)
    ticket = jax.random.randint(jax.random.fold_in(stream_key, 1), dims, 0, int(grid[count - 1]))
    grade = jnp.searchsorted(jnp.asarray(grid, jnp.int32), ticket, side="right")
    return jax.random.permutation(jax.random.fold_in(stream_key, 2), count)[grade].astype(jnp.int32)


def gaussian(rng, extent, deviation, limit, cuts=(), kind=jnp.bfloat16):
    factor_of = levels(rng, extent, cuts, -0.22, 0.18) if cuts else 1.0
    values = jax.random.normal(rng, extent, jnp.float32) * deviation * factor_of
    return jnp.minimum(jnp.maximum(values, -limit), limit).astype(kind)


def setup_inputs(seed: int = 0) -> dict:
    arg_keys = jax.random.split(jax.random.key(seed), 5)
    displace = gaussian(arg_keys[0], (ROUNDS, NSRC, 2, STEPS, NZ, NH), 1.0, 6.0, ((1, 32), (4, 4)))
    green = gaussian(arg_keys[1], (NREC, 2, 2, STEPS, NZ, NH), 1.0, 6.0, ((0, 32), (4, 4)))
    pair_src = set_ends(skewed_ids(arg_keys[2], (ROUNDS, NREC), NSRC, 2), jax.random.fold_in(arg_keys[2], 3), 0, NSRC - 1).astype(jnp.int32)
    source_at = jax.vmap(lambda own: jax.random.permutation(own, NSRC))(jax.random.split(arg_keys[3], ROUNDS)).reshape((ROUNDS, NSRC)).astype(jnp.int32)
    return dict(displace=displace, green=green, pair_src=pair_src, source_at=source_at)


def strain_of(padded, heights):
    def ddx(v):
        return (jnp.roll(v, -1, -1) - jnp.roll(v, 1, -1)) * 0.5

    def ddz(v):
        return (v[..., 2:, :] - v[..., :-2, :]) / (2.0 * heights[:, None])

    wx = padded[..., 0, :, :, :]
    wz = padded[..., 1, :, :, :]
    exx = ddx(wx[..., 1:-1, :])
    ezz = ddz(wz)
    exz = 0.5 * (ddz(wx) + ddx(wz[..., 1:-1, :]))
    return jnp.stack([exx, ezz, exz], axis=-4).astype(jnp.bfloat16)


def kernels_of(source_part, green_part):
    steps = source_part.shape[-3]
    div_source = source_part[..., 0, :, :, :] + source_part[..., 1, :, :, :]
    div_green = green_part[..., 0, :, :, :] + green_part[..., 1, :, :, :]
    weights = jnp.array([2.0, 2.0, 4.0], dtype=jnp.float32)[:, None, None, None]
    weighted = source_part * weights
    lam_list = []
    shear_list = []
    for lag in range(LAGS):
        offset = lag - LAGS // 2
        first = max(0, -offset)
        last = min(steps, steps - offset)
        lam_list.append(jnp.sum(div_source[..., first:last, :, :] * div_green[..., first + offset:last + offset, :, :], axis=-3))
        shear_list.append(jnp.sum(weighted[..., first:last, :, :] * green_part[..., first + offset:last + offset, :, :], axis=(-4, -3)))
    lam = jnp.stack(lam_list, axis=-3)
    shear = jnp.stack(shear_list, axis=-3)
    return jnp.stack([lam, shear], axis=-5)


def reference(displace, green, pair_src, source_at):
    depth_total = displace.shape[4]
    rounds = displace.shape[0]
    nsrc = source_at.shape[1]
    rows = jnp.arange(depth_total, dtype=jnp.int32)
    heights = 0.5 + 1.5 * (rows.astype(jnp.float32) + 0.5) / depth_total
    pad_width = ((0, 0), (0, 0), (0, 0), (0, 0), (1, 1), (0, 0))
    source_strain = strain_of(jnp.pad(displace.astype(jnp.float32), pad_width), heights)
    match = pair_src[:, :, None] == jnp.arange(nsrc, dtype=jnp.int32)[None, None, :]
    slots = jnp.sum(jnp.where(match, source_at[:, None, :], 0), axis=2).astype(jnp.int32)
    round_index = jnp.arange(rounds, dtype=jnp.int32)

    def per_receiver(item):
        green_one, slot_col = item
        green_pad = jnp.pad(green_one.astype(jnp.float32), ((0, 0), (0, 0), (0, 0), (1, 1), (0, 0)))
        green_strain = strain_of(green_pad, heights)
        paired = source_strain[round_index, slot_col]
        out = kernels_of(paired.astype(jnp.float32)[:, None], green_strain.astype(jnp.float32)[None])
        return out.astype(jnp.bfloat16)

    result = lax.map(per_receiver, (green, jnp.transpose(slots)))
    return jnp.moveaxis(result, 0, 1)
```

```python
import jax
import jax.numpy as jnp
from jax import lax
from jax.experimental import pallas as pl
from jax.experimental.pallas import tpu as pltpu
from jax.sharding import PartitionSpec as P

LAGS = 9
F32 = jnp.float32
BF16 = jnp.bfloat16
VMEM = pl.BlockSpec(memory_space=pltpu.VMEM)
SMEM = pl.BlockSpec(memory_space=pltpu.SMEM)


def inverse_spacing():
    depth = lax.axis_index("depth")
    total = 8 * lax.axis_size("depth")
    row = (lax.broadcasted_iota(jnp.int32, (8, 128), 0) + depth * 8).astype(F32)
    heights = 0.5 + 1.5 * (row + 0.5) / total
    return 1.0 / (2.0 * heights)


def strain_of(wx, wz, lo_x, hi_x, lo_z, hi_z, inverse, row):
    def ddx(v):
        return (pltpu.roll(v, 127, 1) - pltpu.roll(v, 1, 1)) * 0.5

    def ddz(v, lo, hi):
        after = jnp.where(row == 7, hi, pltpu.roll(v, 7, 0))
        before = jnp.where(row == 0, lo, pltpu.roll(v, 1, 0))
        return (after - before) * inverse

    return ddx(wx), ddz(wz, lo_z, hi_z), 0.5 * (ddz(wx, lo_x, hi_x) + ddx(wz))


def edges_kernel(displace_ref, green_ref, first_ref, second_ref):
    odd = lax.rem(lax.axis_index("depth"), 2) == 1
    base = 0
    for ref in (displace_ref, green_ref):
        for start in range(0, ref.shape[0], 16):
            slabs = ref[start : start + 16].astype(F32)
            top, bottom = slabs[:, 0, :], slabs[:, 7, :]
            first_ref[base + start : base + start + 16] = jnp.where(odd, top, bottom).astype(BF16)
            second_ref[base + start : base + start + 16] = jnp.where(odd, bottom, top).astype(BF16)
        base += ref.shape[0]


def pack_kernel(pair_ref, at_ref, displace_ref, first_ref, second_ref, out_ref):
    rounds, comps, steps = displace_ref.shape[:3]
    odd = lax.rem(lax.axis_index("depth"), 2) == 1
    row = lax.broadcasted_iota(jnp.int32, (8, 128), 0)
    lane = lax.broadcasted_iota(jnp.int32, (8, 128), 1)
    for k in range(rounds):
        extra = jnp.zeros((8, 128), F32)
        for r in range(pair_ref.shape[1]):
            slot = at_ref[k, pair_ref[k, r]].astype(F32)
            extra = jnp.where((row == 4) & (lane == r), slot, extra)
        halos = []
        for c in range(comps):
            at = (k * comps + c) * steps
            one = first_ref[at : at + steps].astype(F32)
            two = second_ref[at : at + steps].astype(F32)
            halos += [jnp.where(odd, one, two), jnp.where(odd, two, one)]
        for t in range(steps):
            p = k * steps + t
            for c in range(comps):
                out_ref[p, c] = displace_ref[k, c, t]
            tile = extra
            for i, halo in enumerate(halos):
                tile = jnp.where(row == i, jnp.broadcast_to(halo[t : t + 1], (8, 128)), tile)
            out_ref[p, 2] = tile.astype(BF16)


def select_kernel(in_ref, out_ref, strain_ref, slots_ref, scalars_ref, sem):
    sources, receivers = in_ref.shape[0], out_ref.shape[1] // 3
    inverse = inverse_spacing()
    row = lax.broadcasted_iota(jnp.int32, (8, 128), 0)
    for s in range(sources):
        slots_ref[s : s + 1] = in_ref[s, 2].astype(F32)[4:5].astype(jnp.int32)
    copy = pltpu.make_async_copy(slots_ref, scalars_ref, sem)
    copy.start()

    def strain_step(s, carry):
        tile = in_ref[s, 2].astype(F32)
        lo_x, hi_x, lo_z, hi_z = (jnp.broadcast_to(tile[i : i + 1], (8, 128)) for i in range(4))
        wx, wz = in_ref[s, 0].astype(F32), in_ref[s, 1].astype(F32)
        for c, part in enumerate(strain_of(wx, wz, lo_x, hi_x, lo_z, hi_z, inverse, row)):
            strain_ref[s, c] = part.astype(BF16)
        return carry

    lax.fori_loop(0, sources, strain_step, 0, unroll=4)
    copy.wait()

    def select_step(d, carry):
        for r in range(receivers):
            s = scalars_ref[d, r]
            for c in range(3):
                out_ref[d, r * 3 + c] = strain_ref[s, c]
        return carry

    lax.fori_loop(0, sources, select_step, 0, unroll=4)


def correlate_kernel(source_ref, green_ref, first_ref, second_ref, out_ref, green_strain_ref):
    forces, comps, steps = green_ref.shape[1:4]

    @pl.when(pl.program_id(1) == 0)
    def _():
        odd = lax.rem(lax.axis_index("depth"), 2) == 1
        inverse = inverse_spacing()
        row = lax.broadcasted_iota(jnp.int32, (8, 128), 0)
        for f in range(forces):
            halos = []
            for c in range(comps):
                at = (f * comps + c) * steps
                one = first_ref[0, at : at + steps].astype(F32)
                two = second_ref[0, at : at + steps].astype(F32)
                halos += [jnp.where(odd, one, two), jnp.where(odd, two, one)]
            for t in range(steps):
                rows = [jnp.broadcast_to(halo[t : t + 1], (8, 128)) for halo in halos]
                wx, wz = green_ref[0, f, 0, t].astype(F32), green_ref[0, f, 1, t].astype(F32)
                b0, b1, b2 = (b.astype(BF16).astype(F32) for b in strain_of(wx, wz, *rows, inverse, row))
                green_strain_ref[f, t, 0] = b0 + b1
                green_strain_ref[f, t, 1] = b0 - b1
                green_strain_ref[f, t, 2] = b2

    total, spread, cross = [], [], []
    for t in range(steps):
        a0, a1, a2 = (source_ref[t, c].astype(F32) for c in range(3))
        total.append(a0 + a1)
        spread.append(a0 - a1)
        cross.append(a2 * 4.0)
    for f in range(forces):
        for lag in range(LAGS):
            offset = lag - LAGS // 2
            lam = shear = None
            for t in range(max(0, -offset), min(steps, steps - offset)):
                u = t + offset
                x = total[t] * green_strain_ref[f, u, 0]
                y = spread[t] * green_strain_ref[f, u, 1] + cross[t] * green_strain_ref[f, u, 2]
                lam = x if lam is None else lam + x
                shear = y if shear is None else shear + y
            out_ref[0, 0, 0, f, lag] = lam.astype(BF16)
            out_ref[0, 0, 1, f, lag] = (lam + shear).astype(BF16)


def shards(displace, green, pair_src, source_at):
    rounds, _, comps, steps, rows, cells = displace.shape
    receivers, forces = green.shape[:2]
    sources = source_at.shape[1]
    assert rounds * steps == lax.axis_size("recv") == sources
    assert (rows, cells, lax.axis_size("depth")) == (8, 128, 4)

    own = rounds * comps * steps
    far = receivers * forces * comps * steps
    edges = jax.ShapeDtypeStruct((own + far, cells), BF16)
    first, second = pl.pallas_call(
        edges_kernel, out_shape=(edges, edges), in_specs=[VMEM] * 2, out_specs=(VMEM, VMEM), name="edges"
    )(displace.reshape(own, rows, cells), green.reshape(far, rows, cells))
    second = lax.ppermute(second, "depth", [(1, 2), (2, 1)])
    first = lax.ppermute(first, "depth", [(0, 1), (1, 0), (2, 3), (3, 2)])

    packed = pl.pallas_call(
        pack_kernel,
        out_shape=jax.ShapeDtypeStruct((sources, 3, rows, cells), BF16),
        in_specs=[SMEM, SMEM, VMEM, VMEM, VMEM],
        out_specs=VMEM,
        name="pack",
    )(pair_src, source_at, displace.reshape(rounds, comps, steps, rows, cells), first, second)
    pieces = lax.all_to_all(packed, "recv", 0, 0, tiled=True)
    chosen = pl.pallas_call(
        select_kernel,
        out_shape=jax.ShapeDtypeStruct((sources, receivers * 3, rows, cells), BF16),
        in_specs=[VMEM],
        out_specs=VMEM,
        scratch_shapes=[
            pltpu.VMEM((sources, 3, rows, cells), BF16),
            pltpu.VMEM((sources, cells), jnp.int32),
            pltpu.SMEM((sources, cells), jnp.int32),
            pltpu.SemaphoreType.DMA,
        ],
        name="select",
    )(pieces)
    paired = lax.all_to_all(chosen, "recv", 0, 0, tiled=True)
    per = forces * comps * steps
    skip = own // per
    halo = pl.BlockSpec((1, per, cells), lambda r, k: (r + skip, 0, 0))
    return pl.pallas_call(
        correlate_kernel,
        grid=(receivers, rounds),
        out_shape=jax.ShapeDtypeStruct((rounds, receivers, 2, forces, LAGS, rows, cells), BF16),
        in_specs=[
            pl.BlockSpec((steps, 3, rows, cells), lambda r, k: (k, r, 0, 0)),
            pl.BlockSpec((1, forces, comps, steps, rows, cells), lambda r, k: (r, 0, 0, 0, 0, 0)),
            halo,
            halo,
        ],
        out_specs=pl.BlockSpec((1, 1, 2, forces, LAGS, rows, cells), lambda r, k: (k, r, 0, 0, 0, 0, 0)),
        scratch_shapes=[pltpu.VMEM((forces, steps, 3, rows, cells), F32)],
        name="correlate",
    )(paired, green, first.reshape(-1, per, cells), second.reshape(-1, per, cells))


def solution(mesh):
    return jax.shard_map(
        shards,
        mesh=mesh,
        in_specs=(
            P(None, "recv", None, None, "depth", None),
            P("recv", None, None, None, "depth", None),
            P(None, "recv"),
            P(),
        ),
        out_specs=P(None, "recv", None, None, None, "depth", None),
        check_vma=False,
    )
```

```python
import jax
import jax.numpy as jnp
from jax import lax
from jax.experimental import pallas as pl
from jax.experimental.pallas import tpu as pltpu
from jax.sharding import PartitionSpec as P

LAGS = 9
F32 = jnp.float32
BF16 = jnp.bfloat16
VMEM = pl.BlockSpec(memory_space=pltpu.VMEM)
SMEM = pl.BlockSpec(memory_space=pltpu.SMEM)
ANY = pl.BlockSpec(memory_space=pl.ANY)
SAME_CHIP = [(0, 1), (1, 0), (2, 3), (3, 2)]
NEXT_CHIP = [(1, 2), (2, 1)]


def pinned(*arrays):
    return [pltpu.with_memory_space_constraint(a, pltpu.VMEM) for a in arrays]


def inverse_spacing():
    depth = lax.axis_index("depth")
    total = 8 * lax.axis_size("depth")
    row = (lax.broadcasted_iota(jnp.int32, (8, 128), 0) + depth * 8).astype(F32)
    heights = 0.5 + 1.5 * (row + 0.5) / total
    return 1.0 / (2.0 * heights)


def is_odd():
    return lax.rem(lax.axis_index("depth"), 2) == 1


def strain_of(wx, wz, lo_x, hi_x, lo_z, hi_z, inverse, row):
    def ddx(v):
        return (pltpu.roll(v, 127, 1) - pltpu.roll(v, 1, 1)) * 0.5

    def ddz(v, lo, hi):
        after = jnp.where(row == 7, hi, pltpu.roll(v, 7, 0))
        before = jnp.where(row == 0, lo, pltpu.roll(v, 1, 0))
        return (after - before) * inverse

    return ddx(wx), ddz(wz, lo_z, hi_z), 0.5 * (ddz(wx, lo_x, hi_x) + ddx(wz))


def wide(row):
    return jnp.broadcast_to(row, (8, 128))


def store_edges(slabs, at, odd, first_ref, second_ref):
    count = slabs.shape[0]
    top, bottom = slabs[:, 0, :], slabs[:, 7, :]
    first_ref[at : at + count] = jnp.where(odd, top, bottom).astype(BF16)
    second_ref[at : at + count] = jnp.where(odd, bottom, top).astype(BF16)


def begin_kernel(pair_ref, at_ref, displace_ref, first_ref, second_ref, out_ref):
    rounds, comps, steps = displace_ref.shape[:3]
    odd = is_odd()
    for k in range(rounds):
        for c in range(comps):
            slabs = displace_ref[k, c].astype(F32)
            store_edges(slabs, (k * comps + c) * steps, odd, first_ref, second_ref)
            for t in range(steps):
                out_ref[k * steps + t, c] = displace_ref[k, c, t]
    row = lax.broadcasted_iota(jnp.int32, (8, 128), 0)
    lane = lax.broadcasted_iota(jnp.int32, (8, 128), 1)
    for k in range(rounds):
        extra = jnp.zeros((8, 128), F32)
        for r in range(pair_ref.shape[1]):
            slot = at_ref[k, pair_ref[k, r]].astype(F32)
            extra = jnp.where((row == 4) & (lane == r), slot, extra)
        for t in range(steps):
            out_ref[k * steps + t, 2] = extra.astype(BF16)


def halos_kernel(first_ref, second_ref, in_ref, out_ref, *, rounds, comps):
    steps = in_ref.shape[0] // rounds
    odd = is_odd()
    row = lax.broadcasted_iota(jnp.int32, (8, 128), 0)
    for k in range(rounds):
        halos = []
        for c in range(comps):
            at = (k * comps + c) * steps
            one, two = first_ref[at : at + steps].astype(F32), second_ref[at : at + steps].astype(F32)
            halos += [jnp.where(odd, one, two), jnp.where(odd, two, one)]
        for t in range(steps):
            p = k * steps + t
            tile = in_ref[p, 2].astype(F32)
            for i, halo in enumerate(halos):
                tile = jnp.where(row == i, wide(halo[t : t + 1]), tile)
            out_ref[p, 2] = tile.astype(BF16)


def select_kernel(in_ref, out_ref, strain_ref, slots_ref, scalars_ref, sem):
    sources, receivers = in_ref.shape[0], out_ref.shape[1] // 3
    for s in range(sources):
        slots_ref[s : s + 1] = in_ref[s, 2].astype(F32)[4:5].astype(jnp.int32)
    copy = pltpu.make_async_copy(slots_ref, scalars_ref, sem)
    copy.start()
    inverse = inverse_spacing()
    row = lax.broadcasted_iota(jnp.int32, (8, 128), 0)

    def strain_step(s, carry):
        tile = in_ref[s, 2].astype(F32)
        halos = [wide(tile[i : i + 1]) for i in range(4)]
        wx, wz = in_ref[s, 0].astype(F32), in_ref[s, 1].astype(F32)
        for c, part in enumerate(strain_of(wx, wz, *halos, inverse, row)):
            strain_ref[s, c] = part.astype(BF16)
        return carry

    lax.fori_loop(0, sources, strain_step, 0, unroll=8)
    copy.wait()

    def select_step(d, carry):
        for r in range(receivers):
            s = scalars_ref[d, r]
            for c in range(3):
                out_ref[d, r * 3 + c] = strain_ref[s, c]
        return carry

    lax.fori_loop(0, sources, select_step, 0, unroll=8)


def green_edges_kernel(green_ref, first_ref, second_ref):
    odd = is_odd()
    for at in range(0, green_ref.shape[0], 8):
        store_edges(green_ref[at : at + 8].astype(F32), at, odd, first_ref, second_ref)


def green_strain_kernel(green_ref, first_ref, second_ref, out_ref):
    pairs, comps, steps = green_ref.shape[:3]
    odd = is_odd()
    inverse = inverse_spacing()
    row = lax.broadcasted_iota(jnp.int32, (8, 128), 0)

    def step(pair, carry):
        halos = []
        for c in range(comps):
            one = first_ref[pair, c].astype(F32)
            two = second_ref[pair, c].astype(F32)
            halos += [jnp.where(odd, one, two), jnp.where(odd, two, one)]
        for t in range(steps):
            rows = [wide(halo[t : t + 1]) for halo in halos]
            wx, wz = green_ref[pair, 0, t].astype(F32), green_ref[pair, 1, t].astype(F32)
            b0, b1, b2 = (b.astype(BF16).astype(F32) for b in strain_of(wx, wz, *rows, inverse, row))
            out_ref[pair, 0, t] = b0 + b1
            out_ref[pair, 1, t] = b0 - b1
            out_ref[pair, 2, t] = b2
        return carry

    lax.fori_loop(0, pairs, step, 0)


def correlate_kernel(source_ref, green_ref, out_ref, buffer_ref, sems):
    rounds, receivers, _, forces = out_ref.shape[:4]
    steps = green_ref.shape[2]

    def leave(k, r):
        i = k * receivers + r
        return pltpu.make_async_copy(buffer_ref.at[i], out_ref.at[k, r], sems.at[i])

    def pair_step(i, carry):
        k, r = i // receivers, lax.rem(i, receivers)
        total, spread, cross = [], [], []
        for t in range(steps):
            a0, a1, a2 = (source_ref[k * steps + t, r * 3 + c].astype(F32) for c in range(3))
            total.append(a0 + a1)
            spread.append(a0 - a1)
            cross.append(a2 * 4.0)
        for f in range(forces):
            g = r * forces + f
            for lag in range(LAGS):
                offset = lag - LAGS // 2
                lam = shear = None
                for t in range(max(0, -offset), min(steps, steps - offset)):
                    u = t + offset
                    x = total[t] * green_ref[g, 0, u]
                    y = spread[t] * green_ref[g, 1, u] + cross[t] * green_ref[g, 2, u]
                    lam = x if lam is None else lam + x
                    shear = y if shear is None else shear + y
                buffer_ref[i, 0, f, lag] = lam.astype(BF16)
                buffer_ref[i, 1, f, lag] = (lam + shear).astype(BF16)
        leave(k, r).start()
        return carry

    lax.fori_loop(0, rounds * receivers, pair_step, 0)
    for i in range(rounds * receivers):
        leave(i // receivers, i % receivers).wait()


def exchange(first, second):
    second = lax.ppermute(second, "depth", NEXT_CHIP)
    first = lax.ppermute(first, "depth", SAME_CHIP)
    return first, second


def shards(displace, green, pair_src, source_at):
    rounds, _, comps, steps, rows, cells = displace.shape
    receivers, forces = green.shape[:2]
    sources = source_at.shape[1]
    assert rounds * steps == lax.axis_size("recv") == sources
    assert (rows, cells, lax.axis_size("depth")) == (8, 128, 4)
    own = rounds * comps * steps
    far = receivers * forces * comps * steps

    first, second, messages = pl.pallas_call(
        begin_kernel,
        out_shape=(
            pltpu.VMEM((own, cells), BF16),
            pltpu.VMEM((own, cells), BF16),
            pltpu.VMEM((sources, 3, rows, cells), BF16),
        ),
        in_specs=[SMEM, SMEM, VMEM],
        out_specs=(VMEM,) * 3,
        name="begin",
    )(pair_src, source_at, displace.reshape(rounds, comps, steps, rows, cells))
    first, second = exchange(first, second)
    messages = pl.pallas_call(
        lambda *refs: halos_kernel(*refs, rounds=rounds, comps=comps),
        out_shape=pltpu.VMEM((sources, 3, rows, cells), BF16),
        in_specs=[VMEM] * 3,
        out_specs=VMEM,
        input_output_aliases={2: 0},
        name="halos",
    )(*pinned(first, second, messages))
    pieces = lax.all_to_all(messages, "recv", 0, 0, tiled=True)

    green_first, green_second = pl.pallas_call(
        green_edges_kernel,
        out_shape=(pltpu.VMEM((far, cells), BF16),) * 2,
        in_specs=[VMEM],
        out_specs=(VMEM,) * 2,
        cost_estimate=pl.CostEstimate(flops=1 << 20, bytes_accessed=1 << 20, transcendentals=0),
        name="green_edges",
    )(green.reshape(far, rows, cells))
    green_first, green_second = exchange(green_first, green_second)
    pairs = receivers * forces
    green_strain = pl.pallas_call(
        green_strain_kernel,
        out_shape=pltpu.VMEM((pairs, 3, steps, rows, cells), F32),
        in_specs=[VMEM] * 3,
        out_specs=VMEM,
        cost_estimate=pl.CostEstimate(flops=1 << 23, bytes_accessed=1 << 20, transcendentals=0),
        name="green_strain",
    )(
        green.reshape(pairs, comps, steps, rows, cells),
        *pinned(*(a.reshape(pairs, comps, steps, cells) for a in (green_first, green_second))),
    )

    chosen = pl.pallas_call(
        select_kernel,
        out_shape=pltpu.VMEM((sources, receivers * 3, rows, cells), BF16),
        in_specs=[VMEM],
        out_specs=VMEM,
        scratch_shapes=[
            pltpu.VMEM((sources, 3, rows, cells), BF16),
            pltpu.VMEM((sources, cells), jnp.int32),
            pltpu.SMEM((sources, cells), jnp.int32),
            pltpu.SemaphoreType.DMA,
        ],
        name="select",
    )(*pinned(pieces))
    paired = lax.all_to_all(chosen, "recv", 0, 0, tiled=True)
    result = (2, forces, LAGS, rows, cells)
    return pl.pallas_call(
        correlate_kernel,
        out_shape=jax.ShapeDtypeStruct((rounds, receivers, *result), BF16),
        in_specs=[VMEM] * 2,
        out_specs=ANY,
        scratch_shapes=[
            pltpu.VMEM((rounds * receivers, *result), BF16),
            pltpu.SemaphoreType.DMA((rounds * receivers,)),
        ],
        name="correlate",
    )(*pinned(paired, green_strain))


def solution(mesh):
    return jax.shard_map(
        shards,
        mesh=mesh,
        in_specs=(
            P(None, "recv", None, None, "depth", None),
            P("recv", None, None, None, "depth", None),
            P(None, "recv"),
            P(),
        ),
        out_specs=P(None, "recv", None, None, None, "depth", None),
        check_vma=False,
    )
```

```python
import jax
import jax.numpy as jnp
from jax import lax
from jax.experimental import pallas as pl
from jax.experimental.pallas import tpu as pltpu
from jax.sharding import PartitionSpec as P

LAGS = 9
FIRST_ORDER = 31
SECOND_ORDER = 22
F32 = jnp.float32
BF16 = jnp.bfloat16
VMEM = pl.BlockSpec(memory_space=pltpu.VMEM)
SMEM = pl.BlockSpec(memory_space=pltpu.SMEM)
ANY = pl.BlockSpec(memory_space=pl.ANY)
SAME_CHIP = [(0, 1), (1, 0), (2, 3), (3, 2)]
NEXT_CHIP = [(1, 2), (2, 1)]


def pinned(*arrays):
    return [pltpu.with_memory_space_constraint(a, pltpu.VMEM) for a in arrays]


def inverse_spacing():
    depth = lax.axis_index("depth")
    total = 8 * lax.axis_size("depth")
    row = (lax.broadcasted_iota(jnp.int32, (8, 128), 0) + depth * 8).astype(F32)
    heights = 0.5 + 1.5 * (row + 0.5) / total
    return 1.0 / (2.0 * heights)


def is_odd():
    return lax.rem(lax.axis_index("depth"), 2) == 1


def strain_of(wx, wz, lo_x, hi_x, lo_z, hi_z, inverse, row):
    def ddx(v):
        return (pltpu.roll(v, 127, 1) - pltpu.roll(v, 1, 1)) * 0.5

    def ddz(v, lo, hi):
        after = jnp.where(row == 7, hi, pltpu.roll(v, 7, 0))
        before = jnp.where(row == 0, lo, pltpu.roll(v, 1, 0))
        return (after - before) * inverse

    return ddx(wx), ddz(wz, lo_z, hi_z), 0.5 * (ddz(wx, lo_x, hi_x) + ddx(wz))


def wide(row):
    return jnp.broadcast_to(row, (8, 128))


def store_edges(slabs, at, odd, first_ref, second_ref):
    count = slabs.shape[0]
    top, bottom = slabs[:, 0, :], slabs[:, 7, :]
    first_ref[at : at + count] = jnp.where(odd, top, bottom).astype(BF16)
    second_ref[at : at + count] = jnp.where(odd, bottom, top).astype(BF16)


def begin_kernel(pair_ref, at_ref, displace_ref, green_ref, first_ref, second_ref, out_ref):
    rounds, comps, steps = displace_ref.shape[:3]
    odd = is_odd()
    for k in range(rounds):
        for c in range(comps):
            slabs = displace_ref[k, c].astype(F32)
            store_edges(slabs, (k * comps + c) * steps, odd, first_ref, second_ref)
            for t in range(steps):
                out_ref[(k * steps + t) ^ FIRST_ORDER, c] = displace_ref[k, c, t]
    base = rounds * comps * steps
    for at in range(0, green_ref.shape[0], 8):
        store_edges(green_ref[at : at + 8].astype(F32), base + at, odd, first_ref, second_ref)
    row = lax.broadcasted_iota(jnp.int32, (8, 128), 0)
    lane = lax.broadcasted_iota(jnp.int32, (8, 128), 1)
    for k in range(rounds):
        extra = jnp.zeros((8, 128), F32)
        for r in range(pair_ref.shape[1]):
            slot = (at_ref[k, pair_ref[k, r]] ^ FIRST_ORDER).astype(F32)
            extra = jnp.where((row == 4) & (lane == r), slot, extra)
        for t in range(steps):
            out_ref[(k * steps + t) ^ FIRST_ORDER, 2] = extra.astype(BF16)


def halos_kernel(first_ref, second_ref, in_ref, out_ref, *, rounds, comps):
    steps = in_ref.shape[0] // rounds
    odd = is_odd()
    row = lax.broadcasted_iota(jnp.int32, (8, 128), 0)
    for k in range(rounds):
        halos = []
        for c in range(comps):
            at = (k * comps + c) * steps
            one, two = first_ref[at : at + steps].astype(F32), second_ref[at : at + steps].astype(F32)
            halos += [jnp.where(odd, one, two), jnp.where(odd, two, one)]
        for t in range(steps):
            p = (k * steps + t) ^ FIRST_ORDER
            tile = in_ref[p, 2].astype(F32)
            for i, halo in enumerate(halos):
                tile = jnp.where(row == i, wide(halo[t : t + 1]), tile)
            out_ref[p, 2] = tile.astype(BF16)


def green_strain(green_ref, first_ref, second_ref, out_ref, inverse, row):
    pairs, comps, steps = green_ref.shape[:3]
    skip = first_ref.shape[0] - pairs * comps * steps
    odd = is_odd()

    def step(pair, carry):
        halos = []
        for c in range(comps):
            at = pl.multiple_of(skip + (pair * comps + c) * steps, steps)
            one, two = first_ref[pl.ds(at, steps)].astype(F32), second_ref[pl.ds(at, steps)].astype(F32)
            halos += [jnp.where(odd, one, two), jnp.where(odd, two, one)]
        for t in range(steps):
            rows = [wide(halo[t : t + 1]) for halo in halos]
            wx, wz = green_ref[pair, 0, t].astype(F32), green_ref[pair, 1, t].astype(F32)
            for c, part in enumerate(strain_of(wx, wz, *rows, inverse, row)):
                out_ref[pair, c, t] = part.astype(BF16)
        return carry

    lax.fori_loop(0, pairs, step, 0)


def select_kernel(in_ref, green_ref, first_ref, second_ref, out_ref, green_out_ref, strain_ref, slots_ref, scalars_ref, sem):
    sources, receivers = in_ref.shape[0], out_ref.shape[1] // 3
    for s in range(sources):
        slots_ref[s : s + 1] = in_ref[s, 2].astype(F32)[4:5].astype(jnp.int32)
    copy = pltpu.make_async_copy(slots_ref, scalars_ref, sem)
    copy.start()
    inverse = inverse_spacing()
    row = lax.broadcasted_iota(jnp.int32, (8, 128), 0)

    def strain_step(s, carry):
        tile = in_ref[s, 2].astype(F32)
        halos = [wide(tile[i : i + 1]) for i in range(4)]
        wx, wz = in_ref[s, 0].astype(F32), in_ref[s, 1].astype(F32)
        for c, part in enumerate(strain_of(wx, wz, *halos, inverse, row)):
            strain_ref[s, c] = part.astype(BF16)
        return carry

    lax.fori_loop(0, sources, strain_step, 0, unroll=8)
    green_strain(green_ref, first_ref, second_ref, green_out_ref, inverse, row)
    copy.wait()

    def select_step(d, carry):
        for r in range(receivers):
            s = scalars_ref[d ^ (FIRST_ORDER ^ SECOND_ORDER), r]
            for c in range(3):
                out_ref[d, r * 3 + c] = strain_ref[s, c]
        return carry

    lax.fori_loop(0, sources, select_step, 0, unroll=8)


def correlate_kernel(source_ref, strain_ref, out_ref, green_ref, buffer_ref, sems):
    rounds, receivers, _, forces = out_ref.shape[:4]
    steps = green_ref.shape[2]

    def widen(g, carry):
        for t in range(steps):
            b0, b1, b2 = (strain_ref[g, c, t].astype(F32) for c in range(3))
            green_ref[g, 0, t] = b0 + b1
            green_ref[g, 1, t] = b0 - b1
            green_ref[g, 2, t] = b2
        return carry

    lax.fori_loop(0, receivers * forces, widen, 0)

    def leave(k, r):
        i = k * receivers + r
        return pltpu.make_async_copy(buffer_ref.at[i], out_ref.at[k, r], sems.at[i])

    def pair_step(i, carry):
        k, r = i // receivers, lax.rem(i, receivers)
        total, spread, cross = [], [], []
        for t in range(steps):
            a0, a1, a2 = (source_ref[(k * steps + t) ^ SECOND_ORDER, r * 3 + c].astype(F32) for c in range(3))
            total.append(a0 + a1)
            spread.append(a0 - a1)
            cross.append(a2 * 4.0)
        for f in range(forces):
            g = r * forces + f
            for lag in range(LAGS):
                offset = lag - LAGS // 2
                lam = shear = None
                for t in range(max(0, -offset), min(steps, steps - offset)):
                    u = t + offset
                    x = total[t] * green_ref[g, 0, u]
                    y = spread[t] * green_ref[g, 1, u] + cross[t] * green_ref[g, 2, u]
                    lam = x if lam is None else lam + x
                    shear = y if shear is None else shear + y
                buffer_ref[i, 0, f, lag] = lam.astype(BF16)
                buffer_ref[i, 1, f, lag] = (lam + shear).astype(BF16)
        leave(k, r).start()
        return carry

    lax.fori_loop(0, rounds * receivers, pair_step, 0)
    for i in range(rounds * receivers):
        leave(i // receivers, i % receivers).wait()


def exchange(first, second):
    second = lax.ppermute(second, "depth", NEXT_CHIP)
    first = lax.ppermute(first, "depth", SAME_CHIP)
    return first, second


def exchange_all(messages, order):
    groups = [[i ^ order for i in range(messages.shape[0])]]
    return lax.all_to_all(messages, "recv", 0, 0, tiled=True, axis_index_groups=groups)


def shards(displace, green, pair_src, source_at):
    rounds, _, comps, steps, rows, cells = displace.shape
    receivers, forces = green.shape[:2]
    sources = source_at.shape[1]
    assert rounds * steps == lax.axis_size("recv") == sources
    assert (rows, cells, lax.axis_size("depth")) == (8, 128, 4)
    own = rounds * comps * steps
    far = receivers * forces * comps * steps

    first, second, messages = pl.pallas_call(
        begin_kernel,
        out_shape=(
            pltpu.VMEM((own + far, cells), BF16),
            pltpu.VMEM((own + far, cells), BF16),
            pltpu.VMEM((sources, 3, rows, cells), BF16),
        ),
        in_specs=[SMEM, SMEM, VMEM, VMEM],
        out_specs=(VMEM,) * 3,
        name="begin",
    )(pair_src, source_at, displace.reshape(rounds, comps, steps, rows, cells), green.reshape(far, rows, cells))
    first, second = exchange(first, second)
    messages = pl.pallas_call(
        lambda *refs: halos_kernel(*refs, rounds=rounds, comps=comps),
        out_shape=pltpu.VMEM((sources, 3, rows, cells), BF16),
        in_specs=[VMEM] * 3,
        out_specs=VMEM,
        input_output_aliases={2: 0},
        name="halos",
    )(*pinned(first, second, messages))
    pieces = exchange_all(messages, FIRST_ORDER)

    pairs = receivers * forces
    chosen, strain = pl.pallas_call(
        select_kernel,
        out_shape=(
            pltpu.VMEM((sources, receivers * 3, rows, cells), BF16),
            pltpu.VMEM((pairs, 3, steps, rows, cells), BF16),
        ),
        in_specs=[VMEM] * 4,
        out_specs=(VMEM,) * 2,
        scratch_shapes=[
            pltpu.VMEM((sources, 3, rows, cells), BF16),
            pltpu.VMEM((sources, cells), jnp.int32),
            pltpu.SMEM((sources, cells), jnp.int32),
            pltpu.SemaphoreType.DMA,
        ],
        name="select",
    )(*pinned(pieces, green.reshape(pairs, comps, steps, rows, cells), first, second))
    paired = exchange_all(chosen, SECOND_ORDER)
    result = (2, forces, LAGS, rows, cells)
    return pl.pallas_call(
        correlate_kernel,
        out_shape=jax.ShapeDtypeStruct((rounds, receivers, *result), BF16),
        in_specs=[VMEM] * 2,
        out_specs=ANY,
        scratch_shapes=[
            pltpu.VMEM((pairs, 3, steps, rows, cells), F32),
            pltpu.VMEM((rounds * receivers, *result), BF16),
            pltpu.SemaphoreType.DMA((rounds * receivers,)),
        ],
        name="correlate",
    )(*pinned(paired, strain))


def solution(mesh):
    return jax.shard_map(
        shards,
        mesh=mesh,
        in_specs=(
            P(None, "recv", None, None, "depth", None),
            P("recv", None, None, None, "depth", None),
            P(None, "recv"),
            P(),
        ),
        out_specs=P(None, "recv", None, None, None, "depth", None),
        check_vma=False,
    )
```

```python
import jax
import jax.numpy as jnp
from jax import lax
from jax.experimental import pallas as pl
from jax.experimental.pallas import tpu as pltpu
from jax.sharding import PartitionSpec as P

LAGS = 9
FIRST_ORDER = 31
SECOND_ORDER = 22
F32 = jnp.float32
BF16 = jnp.bfloat16
VMEM = pl.BlockSpec(memory_space=pltpu.VMEM)
SMEM = pl.BlockSpec(memory_space=pltpu.SMEM)
ANY = pl.BlockSpec(memory_space=pl.ANY)
SAME_CHIP = [(0, 1), (1, 0), (2, 3), (3, 2)]
NEXT_CHIP = [(1, 2), (2, 1)]


def pinned(*arrays):
    return [pltpu.with_memory_space_constraint(a, pltpu.VMEM) for a in arrays]


def inverse_spacing():
    depth = lax.axis_index("depth")
    total = 8 * lax.axis_size("depth")
    row = (lax.broadcasted_iota(jnp.int32, (8, 128), 0) + depth * 8).astype(F32)
    heights = 0.5 + 1.5 * (row + 0.5) / total
    return 1.0 / (2.0 * heights)


def is_odd():
    return lax.rem(lax.axis_index("depth"), 2) == 1


def strain_of(wx, wz, lo_x, hi_x, lo_z, hi_z, inverse, row):
    def ddx(v):
        return (pltpu.roll(v, 127, 1) - pltpu.roll(v, 1, 1)) * 0.5

    def ddz(v, lo, hi):
        after = jnp.where(row == 7, hi, pltpu.roll(v, 7, 0))
        before = jnp.where(row == 0, lo, pltpu.roll(v, 1, 0))
        return (after - before) * inverse

    return ddx(wx), ddz(wz, lo_z, hi_z), 0.5 * (ddz(wx, lo_x, hi_x) + ddx(wz))


def wide(row):
    return jnp.broadcast_to(row, (8, 128))


def edges_kernel(displace_ref, green_ref, first_ref, second_ref, wide_ref):
    height = displace_ref.shape[1]
    near = jnp.where(is_odd(), 0, height - 1)
    base = 0
    for ref in (displace_ref, green_ref):
        for at in range(0, ref.shape[0], 8):
            start = (base + at) * height
            wide_ref[start : start + 8 * height] = ref[at : at + 8].astype(F32).reshape(8 * height, -1)
            for side, out_ref in ((near, first_ref), (height - 1 - near, second_ref)):
                out_ref[base + at : base + at + 8] = wide_ref[pl.ds(start + side, 8, stride=height)].astype(BF16)
        base += ref.shape[0]


def pack_kernel(pair_ref, at_ref, displace_ref, out_ref):
    rounds, comps, steps = displace_ref.shape[:3]
    row = lax.broadcasted_iota(jnp.int32, (8, 128), 0)
    lane = lax.broadcasted_iota(jnp.int32, (8, 128), 1)
    for k in range(rounds):
        extra = jnp.zeros((8, 128), F32)
        for r in range(pair_ref.shape[1]):
            slot = (at_ref[k, pair_ref[k, r]] ^ FIRST_ORDER).astype(F32)
            extra = jnp.where((row == 4) & (lane == r), slot, extra)
        for t in range(steps):
            p = (k * steps + t) ^ FIRST_ORDER
            for c in range(comps):
                out_ref[p, c] = displace_ref[k, c, t]
            out_ref[p, 2] = extra.astype(BF16)


def halos_kernel(first_ref, second_ref, in_ref, out_ref, *, rounds, comps):
    steps = in_ref.shape[0] // rounds
    odd = is_odd()
    row = lax.broadcasted_iota(jnp.int32, (8, 128), 0)
    for k in range(rounds):
        halos = []
        for c in range(comps):
            at = (k * comps + c) * steps
            one, two = first_ref[at : at + steps].astype(F32), second_ref[at : at + steps].astype(F32)
            halos += [jnp.where(odd, one, two), jnp.where(odd, two, one)]
        for t in range(steps):
            p = (k * steps + t) ^ FIRST_ORDER
            tile = in_ref[p, 2].astype(F32)
            for i, halo in enumerate(halos):
                tile = jnp.where(row == i, wide(halo[t : t + 1]), tile)
            out_ref[p, 2] = tile.astype(BF16)


def green_strain(green_ref, first_ref, second_ref, out_ref, inverse, row):
    pairs, comps, steps = green_ref.shape[:3]
    skip = first_ref.shape[0] - pairs * comps * steps
    odd = is_odd()

    def step(pair, carry):
        halos = []
        for c in range(comps):
            at = pl.multiple_of(skip + (pair * comps + c) * steps, steps)
            one, two = first_ref[pl.ds(at, steps)].astype(F32), second_ref[pl.ds(at, steps)].astype(F32)
            halos += [jnp.where(odd, one, two), jnp.where(odd, two, one)]
        for t in range(steps):
            rows = [wide(halo[t : t + 1]) for halo in halos]
            wx, wz = green_ref[pair, 0, t].astype(F32), green_ref[pair, 1, t].astype(F32)
            for c, part in enumerate(strain_of(wx, wz, *rows, inverse, row)):
                out_ref[pair, c, t] = part.astype(BF16)
        return carry

    lax.fori_loop(0, pairs, step, 0)


def select_kernel(in_ref, green_ref, first_ref, second_ref, out_ref, green_out_ref, strain_ref, slots_ref, scalars_ref, sem):
    sources, receivers = in_ref.shape[0], out_ref.shape[1] // 3
    for s in range(sources):
        slots_ref[s : s + 1] = in_ref[s, 2].astype(F32)[4:5].astype(jnp.int32)
    copy = pltpu.make_async_copy(slots_ref, scalars_ref, sem)
    copy.start()
    inverse = inverse_spacing()
    row = lax.broadcasted_iota(jnp.int32, (8, 128), 0)

    def strain_step(s, carry):
        tile = in_ref[s, 2].astype(F32)
        halos = [wide(tile[i : i + 1]) for i in range(4)]
        wx, wz = in_ref[s, 0].astype(F32), in_ref[s, 1].astype(F32)
        for c, part in enumerate(strain_of(wx, wz, *halos, inverse, row)):
            strain_ref[s, c] = part.astype(BF16)
        return carry

    lax.fori_loop(0, sources, strain_step, 0, unroll=8)
    green_strain(green_ref, first_ref, second_ref, green_out_ref, inverse, row)
    copy.wait()

    def select_step(d, carry):
        for r in range(receivers):
            s = scalars_ref[d ^ (FIRST_ORDER ^ SECOND_ORDER), r]
            for c in range(3):
                out_ref[d, r * 3 + c] = strain_ref[s, c]
        return carry

    lax.fori_loop(0, sources, select_step, 0, unroll=8)


def correlate_kernel(source_ref, strain_ref, out_ref, green_ref, buffer_ref, sems):
    rounds, receivers, _, forces = out_ref.shape[:4]
    steps = green_ref.shape[2]

    def widen(g, carry):
        for t in range(steps):
            b0, b1, b2 = (strain_ref[g, c, t].astype(F32) for c in range(3))
            green_ref[g, 0, t] = b0 + b1
            green_ref[g, 1, t] = b0 - b1
            green_ref[g, 2, t] = b2
        return carry

    lax.fori_loop(0, receivers * forces, widen, 0)

    def leave(k, r):
        i = k * receivers + r
        return pltpu.make_async_copy(buffer_ref.at[i], out_ref.at[k, r], sems.at[i])

    def pair_step(i, carry):
        k, r = i // receivers, lax.rem(i, receivers)
        total, spread, cross = [], [], []
        for t in range(steps):
            a0, a1, a2 = (source_ref[(k * steps + t) ^ SECOND_ORDER, r * 3 + c].astype(F32) for c in range(3))
            total.append(a0 + a1)
            spread.append(a0 - a1)
            cross.append(a2 * 4.0)
        for f in range(forces):
            g = r * forces + f
            for lag in range(LAGS):
                offset = lag - LAGS // 2
                lam = shear = None
                for t in range(max(0, -offset), min(steps, steps - offset)):
                    u = t + offset
                    x = total[t] * green_ref[g, 0, u]
                    y = spread[t] * green_ref[g, 1, u] + cross[t] * green_ref[g, 2, u]
                    lam = x if lam is None else lam + x
                    shear = y if shear is None else shear + y
                buffer_ref[i, 0, f, lag] = lam.astype(BF16)
                buffer_ref[i, 1, f, lag] = (lam + shear).astype(BF16)
        leave(k, r).start()
        return carry

    lax.fori_loop(0, rounds * receivers, pair_step, 0)
    for i in range(rounds * receivers):
        leave(i // receivers, i % receivers).wait()


def exchange(first, second):
    second = lax.ppermute(second, "depth", NEXT_CHIP)
    first = lax.ppermute(first, "depth", SAME_CHIP)
    return first, second


def exchange_all(messages, order):
    groups = [[i ^ order for i in range(messages.shape[0])]]
    return lax.all_to_all(messages, "recv", 0, 0, tiled=True, axis_index_groups=groups)


def shards(displace, green, pair_src, source_at):
    rounds, _, comps, steps, rows, cells = displace.shape
    receivers, forces = green.shape[:2]
    sources = source_at.shape[1]
    assert rounds * steps == lax.axis_size("recv") == sources
    assert (rows, cells, lax.axis_size("depth")) == (8, 128, 4)
    own = rounds * comps * steps
    far = receivers * forces * comps * steps

    edges = pltpu.VMEM((own + far, cells), BF16)
    first, second = pl.pallas_call(
        edges_kernel,
        out_shape=(edges, edges),
        in_specs=[VMEM] * 2,
        out_specs=(VMEM,) * 2,
        scratch_shapes=[pltpu.VMEM(((own + far) * rows, cells), F32)],
        name="edges",
    )(displace.reshape(own, rows, cells), green.reshape(far, rows, cells))
    first, second = exchange(first, second)
    messages = pl.pallas_call(
        pack_kernel,
        out_shape=pltpu.VMEM((sources, 3, rows, cells), BF16),
        in_specs=[SMEM, SMEM, VMEM],
        out_specs=VMEM,
        cost_estimate=pl.CostEstimate(flops=1 << 22, bytes_accessed=1 << 20, transcendentals=0),
        name="pack",
    )(pair_src, source_at, displace.reshape(rounds, comps, steps, rows, cells))
    messages = pl.pallas_call(
        lambda *refs: halos_kernel(*refs, rounds=rounds, comps=comps),
        out_shape=pltpu.VMEM((sources, 3, rows, cells), BF16),
        in_specs=[VMEM] * 3,
        out_specs=VMEM,
        input_output_aliases={2: 0},
        name="halos",
    )(*pinned(first, second, messages))
    pieces = exchange_all(messages, FIRST_ORDER)

    pairs = receivers * forces
    chosen, strain = pl.pallas_call(
        select_kernel,
        out_shape=(
            pltpu.VMEM((sources, receivers * 3, rows, cells), BF16),
            pltpu.VMEM((pairs, 3, steps, rows, cells), BF16),
        ),
        in_specs=[VMEM] * 4,
        out_specs=(VMEM,) * 2,
        scratch_shapes=[
            pltpu.VMEM((sources, 3, rows, cells), BF16),
            pltpu.VMEM((sources, cells), jnp.int32),
            pltpu.SMEM((sources, cells), jnp.int32),
            pltpu.SemaphoreType.DMA,
        ],
        name="select",
    )(*pinned(pieces, green.reshape(pairs, comps, steps, rows, cells), first, second))
    paired = exchange_all(chosen, SECOND_ORDER)
    result = (2, forces, LAGS, rows, cells)
    return pl.pallas_call(
        correlate_kernel,
        out_shape=jax.ShapeDtypeStruct((rounds, receivers, *result), BF16),
        in_specs=[VMEM] * 2,
        out_specs=ANY,
        scratch_shapes=[
            pltpu.VMEM((pairs, 3, steps, rows, cells), F32),
            pltpu.VMEM((rounds * receivers, *result), BF16),
            pltpu.SemaphoreType.DMA((rounds * receivers,)),
        ],
        name="correlate",
    )(*pinned(paired, strain))


def solution(mesh):
    return jax.shard_map(
        shards,
        mesh=mesh,
        in_specs=(
            P(None, "recv", None, None, "depth", None),
            P("recv", None, None, None, "depth", None),
            P(None, "recv"),
            P(),
        ),
        out_specs=P(None, "recv", None, None, None, "depth", None),
        check_vma=False,
    )
```

```python
import jax
import jax.numpy as jnp
from jax import lax
from jax.experimental import pallas as pl
from jax.experimental.pallas import tpu as pltpu
from jax.sharding import PartitionSpec as P

LAGS = 9
FIRST_ORDER = 23
SECOND_ORDER = 22
F32 = jnp.float32
BF16 = jnp.bfloat16
VMEM = pl.BlockSpec(memory_space=pltpu.VMEM)
SMEM = pl.BlockSpec(memory_space=pltpu.SMEM)
ANY = pl.BlockSpec(memory_space=pl.ANY)
SAME_CHIP = [(0, 1), (1, 0), (2, 3), (3, 2)]
NEXT_CHIP = [(1, 2), (2, 1)]


def pinned(*arrays):
    return [pltpu.with_memory_space_constraint(a, pltpu.VMEM) for a in arrays]


def inverse_spacing():
    depth = lax.axis_index("depth")
    total = 8 * lax.axis_size("depth")
    row = (lax.broadcasted_iota(jnp.int32, (8, 128), 0) + depth * 8).astype(F32)
    heights = 0.5 + 1.5 * (row + 0.5) / total
    return 1.0 / (2.0 * heights)


def is_odd():
    return lax.rem(lax.axis_index("depth"), 2) == 1


def strain_of(wx, wz, lo_x, hi_x, lo_z, hi_z, inverse, row):
    def ddx(v):
        return (pltpu.roll(v, 127, 1) - pltpu.roll(v, 1, 1)) * 0.5

    def ddz(v, lo, hi):
        after = jnp.where(row == 7, hi, pltpu.roll(v, 7, 0))
        before = jnp.where(row == 0, lo, pltpu.roll(v, 1, 0))
        return (after - before) * inverse

    return ddx(wx), ddz(wz, lo_z, hi_z), 0.5 * (ddz(wx, lo_x, hi_x) + ddx(wz))


def wide(row):
    return jnp.broadcast_to(row, (8, 128))


def edges_kernel(displace_ref, green_ref, first_ref, second_ref, wide_ref):
    height = displace_ref.shape[1]
    near = jnp.where(is_odd(), 0, height - 1)
    base = 0
    for ref in (displace_ref, green_ref):
        for at in range(0, ref.shape[0], 8):
            start = (base + at) * height
            wide_ref[start : start + 8 * height] = ref[at : at + 8].astype(F32).reshape(8 * height, -1)
            for side, out_ref in ((near, first_ref), (height - 1 - near, second_ref)):
                out_ref[base + at : base + at + 8] = wide_ref[pl.ds(start + side, 8, stride=height)].astype(BF16)
        base += ref.shape[0]


def pack_kernel(pair_ref, at_ref, displace_ref, out_ref):
    rounds, comps, steps = displace_ref.shape[:3]
    row = lax.broadcasted_iota(jnp.int32, (8, 128), 0)
    lane = lax.broadcasted_iota(jnp.int32, (8, 128), 1)
    for k in range(rounds):
        extra = jnp.zeros((8, 128), F32)
        for r in range(pair_ref.shape[1]):
            slot = (at_ref[k, pair_ref[k, r]] ^ FIRST_ORDER).astype(F32)
            extra = jnp.where((row == 4) & (lane == r), slot, extra)
        for t in range(steps):
            p = (k * steps + t) ^ FIRST_ORDER
            for c in range(comps):
                out_ref[p, c] = displace_ref[k, c, t]
            out_ref[p, 2] = extra.astype(BF16)


def halos_kernel(first_ref, second_ref, in_ref, out_ref, *, rounds, comps):
    steps = in_ref.shape[0] // rounds
    odd = is_odd()
    row = lax.broadcasted_iota(jnp.int32, (8, 128), 0)
    for k in range(rounds):
        halos = []
        for c in range(comps):
            at = (k * comps + c) * steps
            one, two = first_ref[at : at + steps].astype(F32), second_ref[at : at + steps].astype(F32)
            halos += [jnp.where(odd, one, two), jnp.where(odd, two, one)]
        for t in range(steps):
            p = (k * steps + t) ^ FIRST_ORDER
            tile = in_ref[p, 2].astype(F32)
            for i, halo in enumerate(halos):
                tile = jnp.where(row == i, wide(halo[t : t + 1]), tile)
            out_ref[p, 2] = tile.astype(BF16)


def green_strain(green_ref, first_ref, second_ref, out_ref, inverse, row):
    pairs, comps, steps = green_ref.shape[:3]
    skip = first_ref.shape[0] - pairs * comps * steps
    odd = is_odd()

    def step(pair, carry):
        halos = []
        for c in range(comps):
            at = pl.multiple_of(skip + (pair * comps + c) * steps, steps)
            one, two = first_ref[pl.ds(at, steps)].astype(F32), second_ref[pl.ds(at, steps)].astype(F32)
            halos += [jnp.where(odd, one, two), jnp.where(odd, two, one)]
        for t in range(steps):
            rows = [wide(halo[t : t + 1]) for halo in halos]
            wx, wz = green_ref[pair, 0, t].astype(F32), green_ref[pair, 1, t].astype(F32)
            b0, b1, b2 = (b.astype(BF16).astype(F32) for b in strain_of(wx, wz, *rows, inverse, row))
            out_ref[pair, 0, t] = b0 + b1
            out_ref[pair, 1, t] = b0 - b1
            out_ref[pair, 2, t] = b2
        return carry

    lax.fori_loop(0, pairs, step, 0)


def select_kernel(in_ref, green_ref, first_ref, second_ref, out_ref, green_out_ref, strain_ref, slots_ref, scalars_ref, sem):
    sources, receivers = in_ref.shape[0], out_ref.shape[1] // 3
    for s in range(sources):
        slots_ref[s : s + 1] = in_ref[s, 2].astype(F32)[4:5].astype(jnp.int32)
    copy = pltpu.make_async_copy(slots_ref, scalars_ref, sem)
    copy.start()
    inverse = inverse_spacing()
    row = lax.broadcasted_iota(jnp.int32, (8, 128), 0)

    def strain_step(s, carry):
        tile = in_ref[s, 2].astype(F32)
        halos = [wide(tile[i : i + 1]) for i in range(4)]
        wx, wz = in_ref[s, 0].astype(F32), in_ref[s, 1].astype(F32)
        for c, part in enumerate(strain_of(wx, wz, *halos, inverse, row)):
            strain_ref[s, c] = part.astype(BF16)
        return carry

    lax.fori_loop(0, sources, strain_step, 0, unroll=8)
    green_strain(green_ref, first_ref, second_ref, green_out_ref, inverse, row)
    copy.wait()

    def select_step(d, carry):
        for r in range(receivers):
            s = scalars_ref[d ^ (FIRST_ORDER ^ SECOND_ORDER), r]
            for c in range(3):
                out_ref[d, r * 3 + c] = strain_ref[s, c]
        return carry

    lax.fori_loop(0, sources, select_step, 0, unroll=8)


def correlate_kernel(source_ref, green_ref, out_ref, buffer_ref, sems):
    rounds, receivers, _, forces = out_ref.shape[:4]
    steps = green_ref.shape[2]

    def leave(k, r):
        i = k * receivers + r
        return pltpu.make_async_copy(buffer_ref.at[i], out_ref.at[k, r], sems.at[i])

    def pair_step(i, carry):
        k, r = i // receivers, lax.rem(i, receivers)
        total, spread, cross = [], [], []
        for t in range(steps):
            a0, a1, a2 = (source_ref[(k * steps + t) ^ SECOND_ORDER, r * 3 + c].astype(F32) for c in range(3))
            total.append(a0 + a1)
            spread.append(a0 - a1)
            cross.append(a2 * 4.0)
        for f in range(forces):
            g = r * forces + f
            for lag in range(LAGS):
                offset = lag - LAGS // 2
                lam = shear = None
                for t in range(max(0, -offset), min(steps, steps - offset)):
                    u = t + offset
                    x = total[t] * green_ref[g, 0, u]
                    y = spread[t] * green_ref[g, 1, u] + cross[t] * green_ref[g, 2, u]
                    lam = x if lam is None else lam + x
                    shear = y if shear is None else shear + y
                buffer_ref[i, 0, f, lag] = lam.astype(BF16)
                buffer_ref[i, 1, f, lag] = (lam + shear).astype(BF16)
        leave(k, r).start()
        return carry

    lax.fori_loop(0, rounds * receivers, pair_step, 0)
    for i in range(rounds * receivers):
        leave(i // receivers, i % receivers).wait()


def exchange(first, second):
    second = lax.ppermute(second, "depth", NEXT_CHIP)
    first = lax.ppermute(first, "depth", SAME_CHIP)
    return first, second


def exchange_all(messages, order):
    groups = [[i ^ order for i in range(messages.shape[0])]]
    return lax.all_to_all(messages, "recv", 0, 0, tiled=True, axis_index_groups=groups)


def shards(displace, green, pair_src, source_at):
    rounds, _, comps, steps, rows, cells = displace.shape
    receivers, forces = green.shape[:2]
    sources = source_at.shape[1]
    assert rounds * steps == lax.axis_size("recv") == sources
    assert (rows, cells, lax.axis_size("depth")) == (8, 128, 4)
    own = rounds * comps * steps
    far = receivers * forces * comps * steps

    edges = pltpu.VMEM((own + far, cells), BF16)
    first, second = pl.pallas_call(
        edges_kernel,
        out_shape=(edges, edges),
        in_specs=[VMEM] * 2,
        out_specs=(VMEM,) * 2,
        scratch_shapes=[pltpu.VMEM(((own + far) * rows, cells), F32)],
        name="edges",
    )(displace.reshape(own, rows, cells), green.reshape(far, rows, cells))
    first, second = exchange(first, second)
    messages = pl.pallas_call(
        pack_kernel,
        out_shape=pltpu.VMEM((sources, 3, rows, cells), BF16),
        in_specs=[SMEM, SMEM, VMEM],
        out_specs=VMEM,
        cost_estimate=pl.CostEstimate(flops=1 << 22, bytes_accessed=1 << 20, transcendentals=0),
        name="pack",
    )(pair_src, source_at, displace.reshape(rounds, comps, steps, rows, cells))
    messages = pl.pallas_call(
        lambda *refs: halos_kernel(*refs, rounds=rounds, comps=comps),
        out_shape=pltpu.VMEM((sources, 3, rows, cells), BF16),
        in_specs=[VMEM] * 3,
        out_specs=VMEM,
        input_output_aliases={2: 0},
        name="halos",
    )(*pinned(first, second, messages))
    pieces = exchange_all(messages, FIRST_ORDER)

    pairs = receivers * forces
    chosen, strain = pl.pallas_call(
        select_kernel,
        out_shape=(
            pltpu.VMEM((sources, receivers * 3, rows, cells), BF16),
            pltpu.VMEM((pairs, 3, steps, rows, cells), F32),
        ),
        in_specs=[VMEM] * 4,
        out_specs=(VMEM,) * 2,
        scratch_shapes=[
            pltpu.VMEM((sources, 3, rows, cells), BF16),
            pltpu.VMEM((sources, cells), jnp.int32),
            pltpu.SMEM((sources, cells), jnp.int32),
            pltpu.SemaphoreType.DMA,
        ],
        compiler_params=pltpu.CompilerParams(vmem_limit_bytes=8 << 20),
        name="select",
    )(*pinned(pieces, green.reshape(pairs, comps, steps, rows, cells), first, second))
    paired = exchange_all(chosen, SECOND_ORDER)
    result = (2, forces, LAGS, rows, cells)
    return pl.pallas_call(
        correlate_kernel,
        out_shape=jax.ShapeDtypeStruct((rounds, receivers, *result), BF16),
        in_specs=[VMEM] * 2,
        out_specs=ANY,
        scratch_shapes=[
            pltpu.VMEM((rounds * receivers, *result), BF16),
            pltpu.SemaphoreType.DMA((rounds * receivers,)),
        ],
        compiler_params=pltpu.CompilerParams(vmem_limit_bytes=8 << 20),
        name="correlate",
    )(*pinned(paired, strain))


def solution(mesh):
    return jax.shard_map(
        shards,
        mesh=mesh,
        in_specs=(
            P(None, "recv", None, None, "depth", None),
            P("recv", None, None, None, "depth", None),
            P(None, "recv"),
            P(),
        ),
        out_specs=P(None, "recv", None, None, None, "depth", None),
        check_vma=False,
    )
```
